32 devices in a mesh: groups: 2 (over x), ctx: 16 (over z, y, core).
Axes of the slice: x: 2, y: 2, z: 4, core: 2. Of those that a mesh axis runs over, the one named last changes fastest.
Arguments:
- residual: bfloat16 [4096, 2048], P(('groups', 'ctx')), parts along dimension 0, may hold values from -200 to 200
- queries: bfloat16 [4096, 2048], P(('groups', 'ctx')), parts along dimension 0, may hold values from -64 to 64
- keys: bfloat16 [4096, 256], P(('groups', 'ctx')), parts along dimension 0, may hold values from -64 to 64
- values: bfloat16 [4096, 256], P(('groups', 'ctx')), parts along dimension 0, may hold values from -6 to 6
- block_order: int32 [32], P('groups'), parts along dimension 0, may hold values from 0 to 3, as said below
- routes: int32 [4096, 8], P(('groups', 'ctx')), parts along dimension 0, may hold values from 0 to 15, as said below
- route_weights: float32 [4096, 8], P(('groups', 'ctx')), parts along dimension 0, may hold values from 0.1 to 1
- out_weight: bfloat16 [2048, 2048], P(None, 'ctx'), may hold values from -0.125 to 0.125
- norm_gain: float32 [2048], replicated, may hold values from 0.5 to 1.5
- w_gate_up: bfloat16 [16, 2048, 1536], P('ctx'), may hold values from -0.125 to 0.125
- w_down: bfloat16 [16, 768, 2048], P('ctx'), may hold values from -0.21875 to 0.21875
Outputs:
- context: bfloat16 [4096, 2048], P(('groups', 'ctx')), parts along dimension 0
- mixed: bfloat16 [4096, 2048], P(('groups', 'ctx')), parts along dimension 0
The draws below stay inside these ranges and needn't reach their ends.
There are 2 independent parts, one for each index of `groups`. The reference program is written for one: setup_inputs(seed, part) draws one part's arguments, and reference() takes and returns one part's arrays. A program takes and returns all parts, laid end to end along the dimension named above; an argument that names none is the same for every part. Nothing has to cross between parts.
Inputs may be any that keep to these rules, and one draw needn't show every extreme that they name: `block_order`: for each i below 4, the entries at the indices congruent to i modulo 4 hold every number from 0 to 3 once. `routes`: each token names 8 different experts. Among the tokens of one device no expert is named more than 72 times, and some expert is named exactly 72 times by the tokens of every device.
All inputs are finite; a program needn't handle non-finite values.
Results may differ from the reference program's by a relative error of at most 0.005.
Values may be sent and summed in bfloat16 or wider, within the bound.
No kernel may reach another device: no remote copies, remote signals or barrier semaphores. Data moves between devices by JAX's collectives and lax.ppermute only.
A program may use at most 128 MiB of HBM per device.

```python
import jax
import jax.numpy as jnp
from jax import lax

D = 2048
HEAD_SIZE = 128
FF = 768
QUERY_HEADS = 16
KEY_VALUE_HEADS = 2
TOPK = 8
SEQS = 4
DEVICE_TOKENS = 128
EXPERTS = 16
SPAN = 4
PROMPT_LENGTH = 512
TOKEN_COUNT = 2048
MOST = 72
N_CTX = 16


def query_key_pair(key):
    query_key = jax.random.fold_in(key, 11)
    random_key_draw = jax.random.fold_in(key, 12)
    query_rows = jnp.clip(jax.random.normal(query_key, (TOKEN_COUNT, QUERY_HEADS * HEAD_SIZE), jnp.float32), -6.0, 6.0)
    key_row_matrix = jnp.clip(jax.random.normal(random_key_draw, (TOKEN_COUNT, KEY_VALUE_HEADS * HEAD_SIZE), jnp.float32), -6.0, 6.0)
    return (query_rows, key_row_matrix)


def draw_queries(key, part):
    return query_key_pair(key)[0].astype(jnp.bfloat16)


def draw_keys(key, part):
    return query_key_pair(key)[1].astype(jnp.bfloat16)


def draw_residual(key, part):
    values_out = jnp.clip(jax.random.normal(jax.random.fold_in(key, 41), (TOKEN_COUNT, D), jnp.float32), -6.0, 6.0)
    return values_out.astype(jnp.bfloat16)


def draw_block_order(key, part):
    span = TOKEN_COUNT // DEVICE_TOKENS // SEQS
    prompt_key_rows = jax.random.split(jax.random.fold_in(key, 31), SEQS)
    orders = jax.vmap(lambda single: jax.random.permutation(single, span))(prompt_key_rows)
    return orders.T.reshape(-1).astype(jnp.int32)


def draw_routes(key, part):
    blocks = TOKEN_COUNT // DEVICE_TOKENS
    slots = EXPERTS * MOST
    total = DEVICE_TOKENS * TOPK
    favour = jax.random.randint(jax.random.fold_in(key, 21), (EXPERTS,), 0, 4)
    busiest = jax.random.randint(jax.random.fold_in(key, 22), (), 0, EXPERTS)
    favour = jnp.where(jnp.arange(EXPERTS) == busiest, 8, favour)
    slot_ids = jnp.arange(slots)

    def one_block(index):
        block_key = jax.random.fold_in(jax.random.fold_in(key, 23), index)
        noise = jax.random.randint(block_key, (slots,), 0, 65536)
        priority = (favour[slot_ids // MOST] * 65536 + noise) * slots + slot_ids
        unused, picked = lax.top_k(priority, total)
        chosen = jnp.sort(picked) // MOST
        table = chosen.reshape(TOPK, DEVICE_TOKENS).T
        shuffle = jax.random.permutation(jax.random.fold_in(block_key, 1), DEVICE_TOKENS)
        return table[shuffle]
    return jax.vmap(one_block)(jnp.arange(blocks)).reshape(TOKEN_COUNT, TOPK).astype(jnp.int32)


def steps_of(own_key, extent, cuts, smallest, high):
    def one(dim, parts):
        steps = jax.random.uniform(jax.random.fold_in(jax.random.fold_in(own_key, 6), dim), (parts,), jnp.float32, smallest / len(cuts), high / len(cuts))
        return jnp.repeat(jnp.exp(steps), extent[dim] // parts).reshape((-1,) + (1,) * (len(extent) - dim - 1))

    level = one(*cuts[0])
    for cut in cuts[1:]:
        level = level * one(*cut)
    return level


def gaussian(own_key, shape, scale, reach, cuts=(), kind=jnp.bfloat16):
    factor_of = steps_of(own_key, shape, cuts, -0.22, 0.18) if cuts else 1.0
    drawn = jax.random.normal(own_key, shape, jnp.float32) * scale * factor_of
    return jnp.minimum(jnp.maximum(drawn, -reach), reach).astype(kind)


def setup_inputs(seed: int = 0, part: int = 0) -> dict:
    key_list = jax.random.split(jax.random.key(seed), 12)
    own_keys = jax.random.split(jax.random.fold_in(key_list[11], part), 12)
    residual = draw_residual(jax.random.fold_in(jax.random.fold_in(key_list[11], part), 71), part)
    queries = draw_queries(jax.random.fold_in(jax.random.fold_in(key_list[11], part), 71), part)
    keys = draw_keys(jax.random.fold_in(jax.random.fold_in(key_list[11], part), 71), part)
    values = gaussian(own_keys[3], (TOKEN_COUNT, KEY_VALUE_HEADS * HEAD_SIZE), 1.0, 6.0, ((0, 16),))
    block_order = draw_block_order(jax.random.fold_in(jax.random.fold_in(key_list[11], part), 71), part)
    routes = draw_routes(jax.random.fold_in(jax.random.fold_in(key_list[11], part), 71), part)
    route_weights = jnp.clip(0.1 + 0.9 * jax.random.uniform(own_keys[6], (TOKEN_COUNT, TOPK), jnp.float32) ** steps_of(own_keys[6], (TOKEN_COUNT, TOPK), ((0, 16),), -0.2, 0.2), 0.1, 1.0)
    out_weight = gaussian(key_list[7], (QUERY_HEADS * HEAD_SIZE, D), (QUERY_HEADS * HEAD_SIZE) ** -0.5, 0.125, ((1, 16),))
    norm_gain = jnp.clip(1.0 + 0.1 * jax.random.normal(key_list[8], (D,), jnp.float32), 0.5, 1.5)
    w_gate_up = gaussian(key_list[9], (EXPERTS, D, 2 * FF), D ** -0.5, 0.125, ((0, 16),))
    w_down = gaussian(key_list[10], (EXPERTS, FF, D), FF ** -0.5, 0.21875, ((0, 16),))
    return dict(residual=residual, queries=queries, keys=keys, values=values, block_order=block_order, routes=routes, route_weights=route_weights, out_weight=out_weight, norm_gain=norm_gain, w_gate_up=w_gate_up, w_down=w_down)


def attend_prompt(prompt_queries, prompt_key_rows, prompt_value_rows, prompt_positions):
    query_group_width = QUERY_HEADS // KEY_VALUE_HEADS
    gathered_keys = prompt_key_rows.reshape(PROMPT_LENGTH, KEY_VALUE_HEADS, HEAD_SIZE).astype(jnp.float32)
    gathered_values = prompt_value_rows.reshape(PROMPT_LENGTH, KEY_VALUE_HEADS, HEAD_SIZE).astype(jnp.float32)

    def one_block(inputs):
        local_query_block, query_positions = inputs
        query_head_rows = local_query_block.reshape(DEVICE_TOKENS, KEY_VALUE_HEADS, query_group_width, HEAD_SIZE).astype(jnp.float32)
        scores = jnp.einsum('qhgd,khd->hgqk', query_head_rows, gathered_keys) * HEAD_SIZE ** (-0.5)
        visible = prompt_positions[None, :] <= query_positions[:, None]
        scores = jnp.where(visible[None, None], scores, -jnp.inf)
        highest = lax.optimization_barrier(jnp.max(scores, axis=-1, keepdims=True))
        weights = jnp.exp(scores - highest)
        totals = lax.optimization_barrier(jnp.sum(weights, axis=-1, keepdims=True))
        rounded = lax.optimization_barrier(weights.astype(jnp.bfloat16)).astype(jnp.float32)
        summed = jnp.einsum('hgqk,khd->hgqd', rounded, gathered_values) / totals
        return summed.transpose(2, 0, 1, 3).reshape(DEVICE_TOKENS, QUERY_HEADS * HEAD_SIZE).astype(jnp.bfloat16)
    return lax.map(one_block, (prompt_queries.reshape(SPAN, DEVICE_TOKENS, QUERY_HEADS * HEAD_SIZE), prompt_positions.reshape(SPAN, DEVICE_TOKENS)))

def select_rows(array, prompt):
    width = array.shape[-1]
    return array.reshape(SPAN, SEQS, DEVICE_TOKENS, width)[:, prompt].reshape(PROMPT_LENGTH, width)

def reference(residual, queries, keys, values, block_order, routes, route_weights, out_weight, norm_gain, w_gate_up, w_down):
    positions = block_order.astype(jnp.int32)[:, None] * DEVICE_TOKENS + jnp.arange(DEVICE_TOKENS, dtype=jnp.int32)[None, :]
    results = []
    for prompt in range(SEQS):
        prompt_positions = positions.reshape(SPAN, SEQS, DEVICE_TOKENS)[:, prompt].reshape(PROMPT_LENGTH)
        results.append(attend_prompt(select_rows(queries, prompt), select_rows(keys, prompt), select_rows(values, prompt), prompt_positions))
    context = jnp.stack(results, axis=1).reshape(TOKEN_COUNT, QUERY_HEADS * HEAD_SIZE)
    projected = jnp.dot(context, out_weight, preferred_element_type=jnp.float32)
    updated = residual.astype(jnp.float32) + projected
    normed = (updated * lax.rsqrt(lax.optimization_barrier(jnp.mean(updated * updated, axis=-1, keepdims=True)) + 1e-06) * norm_gain).astype(jnp.bfloat16)
    capacity = N_CTX * MOST
    expert_ids = routes.reshape(-1).astype(jnp.int32)
    one_hot = (expert_ids[:, None] == jnp.arange(EXPERTS, dtype=jnp.int32)[None, :]).astype(jnp.int32)
    ranks = lax.optimization_barrier(jnp.sum(jnp.cumsum(one_hot, axis=0) * one_hot, axis=1)) - 1
    target = expert_ids * capacity + ranks
    source_row = jnp.arange(TOKEN_COUNT * TOPK, dtype=jnp.int32) // TOPK
    table = jnp.zeros((EXPERTS * capacity,), jnp.int32).at[target].set(source_row).reshape(EXPERTS, capacity)

    def run_expert(inputs):
        gate_up, down, index_rows = inputs
        rows_in = normed[index_rows]
        both = jnp.dot(rows_in, gate_up, preferred_element_type=jnp.float32)
        hidden = (jax.nn.silu(both[:, :FF]) * both[:, FF:]).astype(jnp.bfloat16)
        return jnp.dot(hidden, down, preferred_element_type=jnp.float32).astype(jnp.bfloat16)
    outputs = lax.map(run_expert, (w_gate_up, w_down, table))
    gathered = outputs.reshape(EXPERTS * capacity, D)[target].reshape(TOKEN_COUNT, TOPK, D)
    gates = route_weights / lax.optimization_barrier(jnp.sum(route_weights, axis=-1, keepdims=True))
    mixed = updated
    for slot in range(TOPK):
        mixed = mixed + gates[:, slot:slot + 1] * gathered[:, slot].astype(jnp.float32)
    return (context, mixed.astype(jnp.bfloat16))
```

```python
import functools

import jax
import jax.numpy as jnp
from jax import lax
from jax.experimental import pallas as pl
from jax.experimental.pallas import tpu as pltpu
from jax.sharding import PartitionSpec as P

D = 2048
HEAD_SIZE = 128
FF = 768
QUERY_HEADS = 16
KEY_VALUE_HEADS = 2
TOPK = 8
SEQS = 4


def shifted(array, axis, by):
    devices = lax.axis_size(axis)
    return lax.ppermute(array, axis, [(i, (i + by) % devices) for i in range(devices)])


def exchanged(
    residual,
    queries,
    keys,
    values,
    block_order,
    routes,
    route_weights,
    out_weight,
    norm_gain,
    w_gate_up,
    w_down,
):
    device_row_count = queries.shape[0]
    query_group_width = QUERY_HEADS // KEY_VALUE_HEADS
    devices = lax.axis_size("ctx")
    cycle_length = devices // SEQS
    own_index = lax.axis_index("ctx")
    full_weight = lax.all_gather(out_weight, "ctx", axis=1, tiled=True)
    query_position = block_order[own_index]
    query_head_rows = (
        queries.reshape(device_row_count, KEY_VALUE_HEADS, query_group_width, HEAD_SIZE)
        .transpose(1, 2, 0, 3)
        .reshape(KEY_VALUE_HEADS, query_group_width * device_row_count, HEAD_SIZE)
    )
    query_offset = jnp.arange(query_group_width * device_row_count) % device_row_count
    key_offset = jnp.arange(device_row_count)
    scale = HEAD_SIZE ** (-0.5)

    def update(carry, key_value_tuple, key_position):
        summed, running_max, totals = carry
        local_key_block = key_value_tuple[0].reshape(device_row_count, KEY_VALUE_HEADS, HEAD_SIZE)
        local_value_block = key_value_tuple[1].reshape(device_row_count, KEY_VALUE_HEADS, HEAD_SIZE)
        scores = (
            jnp.einsum(
                "hqd,khd->hqk", query_head_rows, local_key_block, preferred_element_type=jnp.float32
            )
            * scale
        )
        visible = (
            key_position * device_row_count + key_offset[None, :]
            <= query_position * device_row_count + query_offset[:, None]
        )
        scores = jnp.where(visible[None], scores, -jnp.inf)
        new_max = jnp.maximum(running_max, jnp.max(scores, axis=-1))
        factor = jnp.exp(running_max - new_max)
        weights = jnp.exp(scores - new_max[..., None])
        totals = totals * factor + jnp.sum(weights, axis=-1)
        summed = summed * factor[..., None] + jnp.einsum(
            "hqk,khd->hqd",
            weights.astype(jnp.bfloat16),
            local_value_block,
            preferred_element_type=jnp.float32,
        )
        return (summed, new_max, totals)

    initial = (
        jnp.zeros((KEY_VALUE_HEADS, query_group_width * device_row_count, HEAD_SIZE), jnp.float32),
        jnp.full((KEY_VALUE_HEADS, query_group_width * device_row_count), -jnp.inf, jnp.float32),
        jnp.zeros((KEY_VALUE_HEADS, query_group_width * device_row_count), jnp.float32),
    )
    local_pair = jnp.stack([keys, values])
    carry = update(initial, local_pair, query_position)

    def advance(step, state):
        current, moving = state
        moving = shifted(moving, "ctx", SEQS)
        anchor = jnp.mod(own_index - SEQS * step, devices)
        key_position = block_order[anchor]
        current = lax.cond(
            key_position <= query_position,
            lambda inner: update(inner, moving, key_position),
            lambda inner: inner,
            current,
        )
        return (current, moving)

    carry, passed = lax.fori_loop(1, cycle_length, advance, (carry, local_pair))
    summed, running_max, totals = carry
    context = (
        (summed / totals[..., None])
        .reshape(KEY_VALUE_HEADS, query_group_width, device_row_count, HEAD_SIZE)
        .transpose(2, 0, 1, 3)
        .reshape(device_row_count, QUERY_HEADS * HEAD_SIZE)
        .astype(jnp.bfloat16)
    )
    projected = jnp.dot(context, full_weight, preferred_element_type=jnp.float32)
    updated = residual.astype(jnp.float32) + projected
    normed = (
        updated * lax.rsqrt(jnp.mean(updated * updated, axis=-1, keepdims=True) + 1e-06) * norm_gain
    ).astype(jnp.bfloat16)
    experts = devices * w_gate_up.shape[0]
    capacity = 9 * device_row_count * TOPK // (8 * experts)
    expert_ids = routes.reshape(-1)
    one_hot = (expert_ids[:, None] == jnp.arange(experts, dtype=jnp.int32)[None, :]).astype(
        jnp.int32
    )
    ranks = jnp.sum(jnp.cumsum(one_hot, axis=0) * one_hot, axis=1) - 1
    target = expert_ids * capacity + ranks
    source_row = jnp.arange(device_row_count * TOPK) // TOPK
    outgoing = (
        jnp.zeros((experts * capacity, D), jnp.bfloat16)
        .at[target]
        .set(normed[source_row])
        .reshape(experts, capacity, D)
    )
    arrived = lax.all_to_all(outgoing, "ctx", split_axis=0, concat_axis=0, tiled=True)
    flat = arrived.reshape(-1, D)
    both = jnp.dot(flat, w_gate_up[0], preferred_element_type=jnp.float32)
    hidden = (jax.nn.silu(both[:, :FF]) * both[:, FF:]).astype(jnp.bfloat16)
    result = (
        jnp.dot(hidden, w_down[0], preferred_element_type=jnp.float32)
        .astype(jnp.bfloat16)
        .reshape(arrived.shape)
    )
    returned = lax.all_to_all(result, "ctx", split_axis=0, concat_axis=0, tiled=True)
    gathered = returned.reshape(-1, D)[target].reshape(device_row_count, TOPK, D)
    gates = route_weights / jnp.sum(route_weights, axis=-1, keepdims=True)
    mixed = updated
    for slot in range(TOPK):
        mixed = mixed + gates[:, slot : slot + 1] * gathered[:, slot].astype(jnp.float32)
    return (context, mixed.astype(jnp.bfloat16))


def ring_order(devices):
    chips = devices // 2
    return list(range(0, chips, 2)) + list(range(chips - 1, 0, -2))


def ring_tables(devices):
    order = ring_order(devices)
    place = {chip: at for at, chip in enumerate(order)}
    chips = len(order)

    def along(i, by):
        chip, core = divmod(i, 2)
        return order[(place[chip] + (by if core == 0 else -by)) % chips] * 2 + core

    steps = [(i, along(i, 1)) for i in range(devices)]
    pairs = [(i, i ^ 1) for i in range(devices)]
    source = [[along(i, -s) for s in range(chips)] for i in range(devices)]
    return steps, pairs, source


def attention_kernel(places, q_ref, *refs):
    block_refs, out_ref = refs[:-1], refs[-1]
    rows = q_ref.shape[0]
    width = KEY_VALUE_HEADS * HEAD_SIZE
    group = QUERY_HEADS // KEY_VALUE_HEADS
    row = lax.broadcasted_iota(jnp.int32, (rows, rows), 0)
    column = lax.broadcasted_iota(jnp.int32, (rows, rows), 1)
    visible = jnp.concatenate(
        [places[b] * rows + column <= places[0] * rows + row for b in range(len(block_refs))],
        axis=1,
    )
    scale = HEAD_SIZE ** (-0.5)
    for head in range(QUERY_HEADS):
        at = (head // group) * HEAD_SIZE
        keys = jnp.concatenate([ref[:, at : at + HEAD_SIZE] for ref in block_refs], axis=0)
        values = jnp.concatenate(
            [ref[:, width + at : width + at + HEAD_SIZE] for ref in block_refs], axis=0
        )
        query = q_ref[:, head * HEAD_SIZE : (head + 1) * HEAD_SIZE]
        scores = (
            lax.dot_general(
                query, keys, (((1,), (1,)), ((), ())), preferred_element_type=jnp.float32
            )
            * scale
        )
        scores = jnp.where(visible, scores, -jnp.inf)
        weights = jnp.exp(scores - jnp.max(scores, axis=1, keepdims=True))
        total = jnp.sum(weights, axis=1, keepdims=True)
        summed = jnp.dot(
            weights.astype(jnp.bfloat16), values, preferred_element_type=jnp.float32
        )
        out_ref[:, head * HEAD_SIZE : (head + 1) * HEAD_SIZE] = (summed / total).astype(
            jnp.bfloat16
        )


def attention(places, queries, blocks):
    rows, width = queries.shape
    keys = rows * len(blocks)
    return pl.pallas_call(
        attention_kernel,
        out_shape=jax.ShapeDtypeStruct((rows, width), jnp.bfloat16),
        in_specs=[pl.BlockSpec(memory_space=pltpu.SMEM)]
        + [pl.BlockSpec(memory_space=pltpu.VMEM)] * (1 + len(blocks)),
        out_specs=pl.BlockSpec(memory_space=pltpu.VMEM),
        cost_estimate=pl.CostEstimate(
            flops=4 * rows * keys * width,
            bytes_accessed=4 * rows * width + 2 * sum(b.size for b in blocks),
            transcendentals=rows * keys * QUERY_HEADS,
        ),
        name="attention",
    )(places, queries, *blocks)


def project_kernel(count, columns, context_ref, residual_ref, gain_ref, *refs):
    weight_refs = refs[:count]
    updated_ref, normed_ref, held, sems = refs[count:]
    wide = weight_refs[0].shape[1]
    copies = [
        pltpu.make_async_copy(weight_refs[b], held.at[b], sems.at[b]) for b in range(count)
    ]
    for copy in copies:
        copy.start()
    context = context_ref[...]
    for b, copy in enumerate(copies):
        copy.wait()
        at = pl.ds(pl.multiple_of(columns[b] * wide, wide), wide)
        updated_ref[:, at] = residual_ref[:, at].astype(jnp.float32) + jnp.dot(
            context, held[b], preferred_element_type=jnp.float32
        )
    updated = updated_ref[...]
    mean = jnp.mean(updated * updated, axis=1, keepdims=True)
    normed_ref[...] = (updated * lax.rsqrt(mean + 1e-06) * gain_ref[...]).astype(jnp.bfloat16)


def project(columns, context, residual, gain, weights):
    rows, width = residual.shape
    count = len(weights)
    return pl.pallas_call(
        functools.partial(project_kernel, count),
        out_shape=(
            jax.ShapeDtypeStruct((rows, width), jnp.float32),
            jax.ShapeDtypeStruct((rows, width), jnp.bfloat16),
        ),
        in_specs=[pl.BlockSpec(memory_space=pltpu.SMEM)]
        + [pl.BlockSpec(memory_space=pltpu.VMEM)] * 3
        + [pl.BlockSpec(memory_space=pl.ANY)] * count,
        out_specs=(pl.BlockSpec(memory_space=pltpu.VMEM),) * 2,
        scratch_shapes=[
            pltpu.VMEM((count,) + weights[0].shape, jnp.bfloat16),
            pltpu.SemaphoreType.DMA((count,)),
        ],
        cost_estimate=pl.CostEstimate(
            flops=2 * rows * context.shape[1] * width,
            bytes_accessed=2 * context.shape[1] * width,
            transcendentals=0,
        ),
        name="project",
    )(columns, context, residual, gain.reshape(1, width), *weights)


def expert_kernel(sources, x_ref, y_ref, gates_ref, up_ref, down_ref, own_ref, other_ref, both, act):
    rows = x_ref.shape[0]
    both[:rows] = x_ref[...]
    both[rows:] = y_ref[...]
    gates = gates_ref[...]
    lane = lax.broadcasted_iota(jnp.int32, gates.shape, 1)
    gate = jnp.concatenate(
        [
            jnp.sum(jnp.where(lane == sources[b], gates, 0.0), axis=1, keepdims=True)
            for b in range(2)
        ],
        axis=0,
    )
    tile = 256

    @pl.loop(0, FF // tile)
    def _(step):
        at = pl.multiple_of(step * tile, tile)
        x = both[...]
        g = jnp.dot(x, up_ref[0, :, pl.ds(at, tile)], preferred_element_type=jnp.float32)
        u = jnp.dot(x, up_ref[0, :, pl.ds(FF + at, tile)], preferred_element_type=jnp.float32)
        act[:, pl.ds(at, tile)] = (g / (1.0 + jnp.exp(-g)) * u).astype(jnp.bfloat16)

    wide = 512

    @pl.loop(0, own_ref.shape[1] // wide)
    def _(step):
        at = pl.multiple_of(step * wide, wide)
        out = jnp.dot(act[...], down_ref[0, :, pl.ds(at, wide)], preferred_element_type=jnp.float32)
        out = gate * out.astype(jnp.bfloat16).astype(jnp.float32)
        out = jnp.where(gate > 0.0, out, 0.0)
        own_ref[:, pl.ds(at, wide)] = out[:rows]
        other_ref[:, pl.ds(at, wide)] = out[rows:].astype(jnp.bfloat16)


def expert(sources, x, y, gates, w_gate_up, w_down):
    rows, width = x.shape
    return pl.pallas_call(
        expert_kernel,
        out_shape=(
            jax.ShapeDtypeStruct((rows, width), jnp.float32),
            jax.ShapeDtypeStruct((rows, width), jnp.bfloat16),
        ),
        in_specs=[pl.BlockSpec(memory_space=pltpu.SMEM)]
        + [pl.BlockSpec(memory_space=pltpu.VMEM)] * 5,
        out_specs=(pl.BlockSpec(memory_space=pltpu.VMEM),) * 2,
        scratch_shapes=[
            pltpu.VMEM((2 * rows, width), jnp.bfloat16),
            pltpu.VMEM((2 * rows, FF), jnp.bfloat16),
        ],
        cost_estimate=pl.CostEstimate(
            flops=12 * rows * width * FF,
            bytes_accessed=10 * rows * width,
            transcendentals=2 * rows * FF,
        ),
        name="expert",
    )(sources, x, y, gates, w_gate_up, w_down)


def ringed(
    residual,
    queries,
    keys,
    values,
    block_order,
    routes,
    route_weights,
    out_weight,
    norm_gain,
    w_gate_up,
    w_down,
):
    rows = queries.shape[0]
    devices = lax.axis_size("ctx")
    own_index = lax.axis_index("ctx")
    steps, pairs, source_table = ring_tables(devices)
    count = devices // 2
    own_sources = jnp.asarray(source_table, jnp.int32)[own_index]
    other_sources = jnp.asarray(source_table, jnp.int32)[own_index ^ 1]

    def along(array):
        return lax.ppermute(array, "ctx", steps)

    def across(array):
        return lax.ppermute(array, "ctx", pairs)

    pair = jnp.concatenate([keys, values], axis=1)
    spans = range(devices // SEQS)
    blocks = [pair] + [shifted(pair, "ctx", SEQS * s) for s in spans[1:]]
    places = jnp.stack([block_order[jnp.mod(own_index - SEQS * s, devices)] for s in spans])

    held = [out_weight]
    for _ in range(count - 1):
        held.append(along(held[-1]))
    weights = held + [across(block) for block in held]

    gates = route_weights / jnp.sum(route_weights, axis=-1, keepdims=True)
    named = routes[:, :, None] == jnp.arange(devices, dtype=jnp.int32)
    spread = jnp.sum(jnp.where(named, gates[:, :, None], 0.0), axis=1)
    arrived = lax.all_to_all(spread.T, "ctx", split_axis=0, concat_axis=0, tiled=True).T

    context = attention(places, queries, blocks)
    updated, normed = project(
        jnp.concatenate([own_sources, other_sources]), context, residual, norm_gain, weights
    )

    moving = normed
    summed = None
    first = None
    for step in range(count):
        if step > 0:
            moving = along(moving)
        sources = jnp.stack([own_sources[step], other_sources[step]])
        own, other = expert(sources, moving, across(moving), arrived, w_gate_up, w_down)
        other = across(other)
        if step == 0:
            first = updated + own + other.astype(jnp.float32)
            continue
        total = own + other.astype(jnp.float32)
        if summed is not None:
            total = total + summed.astype(jnp.float32)
        summed = along(total.astype(jnp.bfloat16))
    mixed = first + summed.astype(jnp.float32)
    return (context, mixed.astype(jnp.bfloat16))


def local(*arrays):
    devices = lax.axis_size("ctx")
    held_experts = arrays[9].shape[0]
    if held_experts == 1 and devices <= 2 * TOPK and devices % (2 * SEQS) == 0:
        return ringed(*arrays)
    return exchanged(*arrays)


def solution(mesh):
    placed = (
        P(("groups", "ctx"), None),
        P(("groups", "ctx"), None),
        P(("groups", "ctx"), None),
        P(("groups", "ctx"), None),
        P("groups"),
        P(("groups", "ctx"), None),
        P(("groups", "ctx"), None),
        P(None, "ctx"),
        P(),
        P("ctx", None, None),
        P("ctx", None, None),
    )
    return jax.shard_map(
        local,
        mesh=mesh,
        in_specs=placed,
        out_specs=(P(("groups", "ctx"), None), P(("groups", "ctx"), None)),
        check_vma=False,
    )
```

```python
import functools

import jax
import jax.numpy as jnp
from jax import lax
from jax.experimental import pallas as pl
from jax.experimental.pallas import tpu as pltpu
from jax.sharding import PartitionSpec as P


D = 2048
HEAD_SIZE = 128
FF = 768
QUERY_HEADS = 16
KEY_VALUE_HEADS = 2
TOPK = 8
SEQS = 4
PARTS = 1
SUM_PARTS = 1


def shifted(array, axis, by):
    devices = lax.axis_size(axis)
    return lax.ppermute(array, axis, [(i, (i + by) % devices) for i in range(devices)])


def exchanged(
    residual,
    queries,
    keys,
    values,
    block_order,
    routes,
    route_weights,
    out_weight,
    norm_gain,
    w_gate_up,
    w_down,
):
    device_row_count = queries.shape[0]
    query_group_width = QUERY_HEADS // KEY_VALUE_HEADS
    devices = lax.axis_size("ctx")
    cycle_length = devices // SEQS
    own_index = lax.axis_index("ctx")
    full_weight = lax.all_gather(out_weight, "ctx", axis=1, tiled=True)
    query_position = block_order[own_index]
    query_head_rows = (
        queries.reshape(device_row_count, KEY_VALUE_HEADS, query_group_width, HEAD_SIZE)
        .transpose(1, 2, 0, 3)
        .reshape(KEY_VALUE_HEADS, query_group_width * device_row_count, HEAD_SIZE)
    )
    query_offset = jnp.arange(query_group_width * device_row_count) % device_row_count
    key_offset = jnp.arange(device_row_count)
    scale = HEAD_SIZE ** (-0.5)

    def update(carry, key_value_tuple, key_position):
        summed, running_max, totals = carry
        local_key_block = key_value_tuple[0].reshape(device_row_count, KEY_VALUE_HEADS, HEAD_SIZE)
        local_value_block = key_value_tuple[1].reshape(device_row_count, KEY_VALUE_HEADS, HEAD_SIZE)
        scores = (
            jnp.einsum(
                "hqd,khd->hqk", query_head_rows, local_key_block, preferred_element_type=jnp.float32
            )
            * scale
        )
        visible = (
            key_position * device_row_count + key_offset[None, :]
            <= query_position * device_row_count + query_offset[:, None]
        )
        scores = jnp.where(visible[None], scores, -jnp.inf)
        new_max = jnp.maximum(running_max, jnp.max(scores, axis=-1))
        factor = jnp.exp(running_max - new_max)
        weights = jnp.exp(scores - new_max[..., None])
        totals = totals * factor + jnp.sum(weights, axis=-1)
        summed = summed * factor[..., None] + jnp.einsum(
            "hqk,khd->hqd",
            weights.astype(jnp.bfloat16),
            local_value_block,
            preferred_element_type=jnp.float32,
        )
        return (summed, new_max, totals)

    initial = (
        jnp.zeros((KEY_VALUE_HEADS, query_group_width * device_row_count, HEAD_SIZE), jnp.float32),
        jnp.full((KEY_VALUE_HEADS, query_group_width * device_row_count), -jnp.inf, jnp.float32),
        jnp.zeros((KEY_VALUE_HEADS, query_group_width * device_row_count), jnp.float32),
    )
    local_pair = jnp.stack([keys, values])
    carry = update(initial, local_pair, query_position)

    def advance(step, state):
        current, moving = state
        moving = shifted(moving, "ctx", SEQS)
        anchor = jnp.mod(own_index - SEQS * step, devices)
        key_position = block_order[anchor]
        current = lax.cond(
            key_position <= query_position,
            lambda inner: update(inner, moving, key_position),
            lambda inner: inner,
            current,
        )
        return (current, moving)

    carry, _ = lax.fori_loop(1, cycle_length, advance, (carry, local_pair))
    summed, _, totals = carry
    context = (
        (summed / totals[..., None])
        .reshape(KEY_VALUE_HEADS, query_group_width, device_row_count, HEAD_SIZE)
        .transpose(2, 0, 1, 3)
        .reshape(device_row_count, QUERY_HEADS * HEAD_SIZE)
        .astype(jnp.bfloat16)
    )
    projected = jnp.dot(context, full_weight, preferred_element_type=jnp.float32)
    updated = residual.astype(jnp.float32) + projected
    normed = (
        updated * lax.rsqrt(jnp.mean(updated * updated, axis=-1, keepdims=True) + 1e-06) * norm_gain
    ).astype(jnp.bfloat16)
    experts = devices * w_gate_up.shape[0]
    capacity = 9 * device_row_count * TOPK // (8 * experts)
    expert_ids = routes.reshape(-1)
    one_hot = (expert_ids[:, None] == jnp.arange(experts, dtype=jnp.int32)[None, :]).astype(
        jnp.int32
    )
    ranks = jnp.sum(jnp.cumsum(one_hot, axis=0) * one_hot, axis=1) - 1
    target = expert_ids * capacity + ranks
    source_row = jnp.arange(device_row_count * TOPK) // TOPK
    outgoing = (
        jnp.zeros((experts * capacity, D), jnp.bfloat16)
        .at[target]
        .set(normed[source_row])
        .reshape(experts, capacity, D)
    )
    arrived = lax.all_to_all(outgoing, "ctx", split_axis=0, concat_axis=0, tiled=True)
    flat = arrived.reshape(-1, D)
    both = jnp.dot(flat, w_gate_up[0], preferred_element_type=jnp.float32)
    hidden = (jax.nn.silu(both[:, :FF]) * both[:, FF:]).astype(jnp.bfloat16)
    result = (
        jnp.dot(hidden, w_down[0], preferred_element_type=jnp.float32)
        .astype(jnp.bfloat16)
        .reshape(arrived.shape)
    )
    returned = lax.all_to_all(result, "ctx", split_axis=0, concat_axis=0, tiled=True)
    gathered = returned.reshape(-1, D)[target].reshape(device_row_count, TOPK, D)
    gates = route_weights / jnp.sum(route_weights, axis=-1, keepdims=True)
    mixed = updated
    for slot in range(TOPK):
        mixed = mixed + gates[:, slot : slot + 1] * gathered[:, slot].astype(jnp.float32)
    return (context, mixed.astype(jnp.bfloat16))


def ring_order(devices):
    chips = devices // 2
    return list(range(0, chips, 2)) + list(range(chips - 1, 0, -2))


def ring_tables(devices):
    order = ring_order(devices)
    place = {chip: at for at, chip in enumerate(order)}
    chips = len(order)

    def along(i, by):
        chip, core = divmod(i, 2)
        return order[(place[chip] + by) % chips] * 2 + core

    def turned(i, by):
        return along(i, by if i % 2 == 0 else -by)

    everyone = range(devices)
    return dict(
        up=[(i, along(i, 1)) for i in everyone],
        down=[(i, along(i, -1)) for i in everyone],
        turned=[(i, turned(i, 1)) for i in everyone],
        pair=[(i, i ^ 1) for i in everyone],
        after_up=[[along(i, -s) for s in range(chips)] for i in everyone],
        after_turned=[[turned(i, -s) for s in range(chips)] for i in everyone],
    )


def attention_kernel(count, table, block_order, q_ref, *refs):
    key_refs, value_refs, out_ref = refs[:count], refs[count : 2 * count], refs[2 * count]
    rows = q_ref.shape[0]
    group = QUERY_HEADS // KEY_VALUE_HEADS
    row = lax.broadcasted_iota(jnp.int32, (rows, rows), 0)
    column = lax.broadcasted_iota(jnp.int32, (rows, rows), 1)
    places = [block_order[table[b]] * rows for b in range(count)]
    visible = jnp.concatenate([place + column <= places[0] + row for place in places], axis=1)
    scale = HEAD_SIZE ** (-0.5)
    for head in range(QUERY_HEADS):
        of = slice(head // group * HEAD_SIZE, (head // group + 1) * HEAD_SIZE)
        keys = jnp.concatenate([ref[:, of] for ref in key_refs], axis=0)
        values = jnp.concatenate([ref[:, of] for ref in value_refs], axis=0)
        query = q_ref[:, head * HEAD_SIZE : (head + 1) * HEAD_SIZE]
        scores = (
            lax.dot_general(
                query, keys, (((1,), (1,)), ((), ())), preferred_element_type=jnp.float32
            )
            * scale
        )
        scores = jnp.where(visible, scores, -jnp.inf)
        weights = jnp.exp(scores - jnp.max(scores, axis=1, keepdims=True))
        total = jnp.sum(weights, axis=1, keepdims=True)
        summed = jnp.dot(
            weights.astype(jnp.bfloat16), values, preferred_element_type=jnp.float32
        )
        out_ref[:, head * HEAD_SIZE : (head + 1) * HEAD_SIZE] = (summed / total).astype(
            jnp.bfloat16
        )


def attention(table, block_order, queries, keys, values):
    rows, width = queries.shape
    count = len(keys)
    return pl.pallas_call(
        functools.partial(attention_kernel, count),
        out_shape=jax.ShapeDtypeStruct((rows, width), jnp.bfloat16),
        in_specs=[pl.BlockSpec(memory_space=pltpu.SMEM)] * 2
        + [pl.BlockSpec(memory_space=pltpu.VMEM)] * (1 + 2 * count),
        out_specs=pl.BlockSpec(memory_space=pltpu.VMEM),
        cost_estimate=pl.CostEstimate(
            flops=4 * rows * rows * count * width,
            bytes_accessed=4 * rows * width + 4 * count * keys[0].size,
            transcendentals=rows * rows * count * QUERY_HEADS,
        ),
        name="attention",
    )(table, block_order, queries, *keys, *values)


def partial_kernel(parts, own_ref, other_ref, *refs):
    mine_ref, theirs_ref = refs[-2:]
    rows = own_ref.shape[0]
    out = 0.0
    done = start = 0
    for count in parts:
        blocks = refs[done : done + count]
        done += count
        at = slice(start, start + blocks[0].shape[0])
        start = at.stop
        context = jnp.concatenate([own_ref[:, at], other_ref[:, at]], axis=0)
        weight = jnp.concatenate([block[...] for block in blocks], axis=1)
        out += jnp.dot(context, weight, preferred_element_type=jnp.float32)
    mine_ref[...] = out[:rows]
    theirs_ref[...] = out[rows:]


def partial_product(own, other, parts):
    rows, depth = own.shape
    wide = sum(block.shape[1] for block in parts[0])
    blocks = [block for part in parts for block in part]
    return pl.pallas_call(
        functools.partial(partial_kernel, [len(part) for part in parts]),
        out_shape=(jax.ShapeDtypeStruct((rows, wide), jnp.float32),) * 2,
        in_specs=[pl.BlockSpec(memory_space=pltpu.VMEM)] * (2 + len(blocks)),
        out_specs=(pl.BlockSpec(memory_space=pltpu.VMEM),) * 2,
        cost_estimate=pl.CostEstimate(
            flops=4 * rows * depth * wide,
            bytes_accessed=2 * depth * wide + 4 * rows * depth,
            transcendentals=0,
        ),
        name="partial_product",
    )(own, other, *blocks)


def finish_kernel(wide, parts, skip, table, residual_ref, gain_ref, *refs):
    piece_refs = refs[: -1 - parts]
    updated_ref, normed_refs = refs[-1 - parts], refs[-parts:]
    done = skip
    for ref in piece_refs:
        for at in range(0, ref.shape[1], wide):
            to = pl.ds(pl.multiple_of(table[done] * wide, wide), wide)
            updated_ref[:, to] = residual_ref[:, to].astype(jnp.float32) + ref[:, at : at + wide]
            done += 1
    rows = updated_ref.shape[0] // parts
    for part, ref in enumerate(normed_refs):
        updated = updated_ref[part * rows : (part + 1) * rows]
        mean = jnp.mean(updated * updated, axis=1, keepdims=True)
        ref[...] = (updated * lax.rsqrt(mean + 1e-06) * gain_ref[...]).astype(jnp.bfloat16)


def finish(table, skip, residual, gain, pieces, parts):
    rows, width = residual.shape
    return pl.pallas_call(
        functools.partial(finish_kernel, width // (table.shape[0] - skip), parts, skip),
        out_shape=(jax.ShapeDtypeStruct((rows, width), jnp.float32),)
        + (jax.ShapeDtypeStruct((rows // parts, width), jnp.bfloat16),) * parts,
        in_specs=[pl.BlockSpec(memory_space=pltpu.SMEM)]
        + [pl.BlockSpec(memory_space=pltpu.VMEM)] * (2 + len(pieces)),
        out_specs=(pl.BlockSpec(memory_space=pltpu.VMEM),) * (1 + parts),
        cost_estimate=pl.CostEstimate(
            flops=6 * rows * width, bytes_accessed=12 * rows * width, transcendentals=rows
        ),
        name="finish",
    )(table, residual, gain.reshape(1, width), *pieces)


def ringed(
    residual,
    queries,
    keys,
    values,
    block_order,
    routes,
    route_weights,
    out_weight,
    norm_gain,
    w_gate_up,
    w_down,
):
    rows = queries.shape[0]
    devices = lax.axis_size("ctx")
    own_index = lax.axis_index("ctx")
    ring = ring_tables(devices)
    chips = devices // 2
    half = chips // 2
    spans = range(devices // SEQS)
    turns = [0] + [t for s in range(1, half) for t in (s, chips - s)] + [half]

    def sent(array, way):
        return lax.ppermute(array, "ctx", ring[way])

    table = []
    for i in range(devices):
        columns = [ring["after_up"][i][t] for t in turns]
        table.append([(i - SEQS * s) % devices for s in spans] + columns + [c ^ 1 for c in columns])
    table = jnp.asarray(table, jnp.int32)[own_index]

    key_blocks = [keys] + [shifted(keys, "ctx", SEQS * s) for s in spans[1:]]
    value_blocks = [values] + [shifted(values, "ctx", SEQS * s) for s in spans[1:]]

    gates = route_weights / jnp.sum(route_weights, axis=-1, keepdims=True)
    named = routes[:, :, None] == jnp.arange(devices, dtype=jnp.int32)
    spread = jnp.sum(jnp.where(named, gates[:, :, None], 0.0), axis=1)
    arrived = lax.all_to_all(spread.T, "ctx", split_axis=0, concat_axis=0, tiled=True)

    depth = out_weight.shape[0] // 2
    up = down = whole = (out_weight[:depth], out_weight[depth:])
    rounds = []
    for _ in range(1, half):
        up = tuple(sent(part, "up") for part in up)
        down = tuple(sent(part, "down") for part in down)
        rounds.append([up, down])
    context = attention(table, block_order, queries, key_blocks, value_blocks)
    rounds.append([(sent(up[0], "up"), sent(down[1], "down"))])
    other_context = sent(context, "pair")
    pieces, away = [], []
    early = [whole] + [block for got in rounds[:-2] for block in got]
    for got in [early] + rounds[-2:]:
        mine, theirs = partial_product(context, other_context, list(zip(*got)))
        pieces.append(mine)
        away.append(sent(theirs, "pair"))
    updated, *normed = finish(table, len(spans), residual, norm_gain, pieces + away, PARTS)

    turned = jnp.asarray(ring["after_turned"], jnp.int32)
    order = jnp.stack([turned[own_index], turned[own_index ^ 1]], axis=1)
    gate_rows = arrived[order]
    moving = normed
    summed = None
    for step in range(chips):
        if step > 0:
            moving = [sent(part, "turned") for part in moving]
        both = jnp.concatenate([*moving, *[sent(part, "pair") for part in moving]], axis=0)
        hidden = jnp.dot(both, w_gate_up[0], preferred_element_type=jnp.float32)
        hidden = (jax.nn.silu(hidden[:, :FF]) * hidden[:, FF:]).astype(jnp.bfloat16)
        out = jnp.dot(hidden, w_down[0], preferred_element_type=jnp.float32).astype(jnp.bfloat16)
        gate = gate_rows[step].reshape(2 * rows, 1)
        out = jnp.where(gate > 0.0, gate * out.astype(jnp.float32), 0.0)
        theirs = sent(out[rows:].astype(jnp.bfloat16), "pair")
        total = out[:rows] + theirs.astype(jnp.float32)
        if step == 0:
            first = updated + total
            continue
        totals = jnp.split(total, SUM_PARTS)
        if summed is not None:
            totals = [t + s.astype(jnp.float32) for t, s in zip(totals, summed)]
        summed = [sent(t.astype(jnp.bfloat16), "turned") for t in totals]
    mixed = first + jnp.concatenate(summed).astype(jnp.float32)
    return (context, mixed.astype(jnp.bfloat16))


def local(*arrays):
    devices = lax.axis_size("ctx")
    held_experts = arrays[9].shape[0]
    if held_experts == 1 and devices <= 2 * TOPK and devices % (2 * SEQS) == 0:
        return ringed(*arrays)
    return exchanged(*arrays)


def solution(mesh):
    placed = (
        P(("groups", "ctx"), None),
        P(("groups", "ctx"), None),
        P(("groups", "ctx"), None),
        P(("groups", "ctx"), None),
        P("groups"),
        P(("groups", "ctx"), None),
        P(("groups", "ctx"), None),
        P(None, "ctx"),
        P(),
        P("ctx", None, None),
        P("ctx", None, None),
    )
    return jax.shard_map(
        local,
        mesh=mesh,
        in_specs=placed,
        out_specs=(P(("groups", "ctx"), None), P(("groups", "ctx"), None)),
        check_vma=False,
    )
```

```python
import functools

import jax
import jax.numpy as jnp
from jax import lax
from jax.experimental import pallas as pl
from jax.experimental.pallas import tpu as pltpu
from jax.sharding import PartitionSpec as P


D = 2048
HEAD_SIZE = 128
FF = 768
QUERY_HEADS = 16
KEY_VALUE_HEADS = 2
TOPK = 8
SEQS = 4
PARTS = 1
TAIL = 3


def shifted(array, axis, by):
    devices = lax.axis_size(axis)
    return lax.ppermute(array, axis, [(i, (i + by) % devices) for i in range(devices)])


def exchanged(
    residual,
    queries,
    keys,
    values,
    block_order,
    routes,
    route_weights,
    out_weight,
    norm_gain,
    w_gate_up,
    w_down,
):
    device_row_count = queries.shape[0]
    query_group_width = QUERY_HEADS // KEY_VALUE_HEADS
    devices = lax.axis_size("ctx")
    cycle_length = devices // SEQS
    own_index = lax.axis_index("ctx")
    full_weight = lax.all_gather(out_weight, "ctx", axis=1, tiled=True)
    query_position = block_order[own_index]
    query_head_rows = (
        queries.reshape(device_row_count, KEY_VALUE_HEADS, query_group_width, HEAD_SIZE)
        .transpose(1, 2, 0, 3)
        .reshape(KEY_VALUE_HEADS, query_group_width * device_row_count, HEAD_SIZE)
    )
    query_offset = jnp.arange(query_group_width * device_row_count) % device_row_count
    key_offset = jnp.arange(device_row_count)
    scale = HEAD_SIZE ** (-0.5)

    def update(carry, key_value_tuple, key_position):
        summed, running_max, totals = carry
        local_key_block = key_value_tuple[0].reshape(device_row_count, KEY_VALUE_HEADS, HEAD_SIZE)
        local_value_block = key_value_tuple[1].reshape(device_row_count, KEY_VALUE_HEADS, HEAD_SIZE)
        scores = (
            jnp.einsum(
                "hqd,khd->hqk", query_head_rows, local_key_block, preferred_element_type=jnp.float32
            )
            * scale
        )
        visible = (
            key_position * device_row_count + key_offset[None, :]
            <= query_position * device_row_count + query_offset[:, None]
        )
        scores = jnp.where(visible[None], scores, -jnp.inf)
        new_max = jnp.maximum(running_max, jnp.max(scores, axis=-1))
        factor = jnp.exp(running_max - new_max)
        weights = jnp.exp(scores - new_max[..., None])
        totals = totals * factor + jnp.sum(weights, axis=-1)
        summed = summed * factor[..., None] + jnp.einsum(
            "hqk,khd->hqd",
            weights.astype(jnp.bfloat16),
            local_value_block,
            preferred_element_type=jnp.float32,
        )
        return (summed, new_max, totals)

    initial = (
        jnp.zeros((KEY_VALUE_HEADS, query_group_width * device_row_count, HEAD_SIZE), jnp.float32),
        jnp.full((KEY_VALUE_HEADS, query_group_width * device_row_count), -jnp.inf, jnp.float32),
        jnp.zeros((KEY_VALUE_HEADS, query_group_width * device_row_count), jnp.float32),
    )
    local_pair = jnp.stack([keys, values])
    carry = update(initial, local_pair, query_position)

    def advance(step, state):
        current, moving = state
        moving = shifted(moving, "ctx", SEQS)
        anchor = jnp.mod(own_index - SEQS * step, devices)
        key_position = block_order[anchor]
        current = lax.cond(
            key_position <= query_position,
            lambda inner: update(inner, moving, key_position),
            lambda inner: inner,
            current,
        )
        return (current, moving)

    carry, _ = lax.fori_loop(1, cycle_length, advance, (carry, local_pair))
    summed, _, totals = carry
    context = (
        (summed / totals[..., None])
        .reshape(KEY_VALUE_HEADS, query_group_width, device_row_count, HEAD_SIZE)
        .transpose(2, 0, 1, 3)
        .reshape(device_row_count, QUERY_HEADS * HEAD_SIZE)
        .astype(jnp.bfloat16)
    )
    projected = jnp.dot(context, full_weight, preferred_element_type=jnp.float32)
    updated = residual.astype(jnp.float32) + projected
    normed = (
        updated * lax.rsqrt(jnp.mean(updated * updated, axis=-1, keepdims=True) + 1e-06) * norm_gain
    ).astype(jnp.bfloat16)
    experts = devices * w_gate_up.shape[0]
    capacity = 9 * device_row_count * TOPK // (8 * experts)
    expert_ids = routes.reshape(-1)
    one_hot = (expert_ids[:, None] == jnp.arange(experts, dtype=jnp.int32)[None, :]).astype(
        jnp.int32
    )
    ranks = jnp.sum(jnp.cumsum(one_hot, axis=0) * one_hot, axis=1) - 1
    target = expert_ids * capacity + ranks
    source_row = jnp.arange(device_row_count * TOPK) // TOPK
    outgoing = (
        jnp.zeros((experts * capacity, D), jnp.bfloat16)
        .at[target]
        .set(normed[source_row])
        .reshape(experts, capacity, D)
    )
    arrived = lax.all_to_all(outgoing, "ctx", split_axis=0, concat_axis=0, tiled=True)
    flat = arrived.reshape(-1, D)
    both = jnp.dot(flat, w_gate_up[0], preferred_element_type=jnp.float32)
    hidden = (jax.nn.silu(both[:, :FF]) * both[:, FF:]).astype(jnp.bfloat16)
    result = (
        jnp.dot(hidden, w_down[0], preferred_element_type=jnp.float32)
        .astype(jnp.bfloat16)
        .reshape(arrived.shape)
    )
    returned = lax.all_to_all(result, "ctx", split_axis=0, concat_axis=0, tiled=True)
    gathered = returned.reshape(-1, D)[target].reshape(device_row_count, TOPK, D)
    gates = route_weights / jnp.sum(route_weights, axis=-1, keepdims=True)
    mixed = updated
    for slot in range(TOPK):
        mixed = mixed + gates[:, slot : slot + 1] * gathered[:, slot].astype(jnp.float32)
    return (context, mixed.astype(jnp.bfloat16))


def ring_order(devices):
    chips = devices // 2
    return list(range(0, chips, 2)) + list(range(chips - 1, 0, -2))


def ring_tables(devices):
    order = ring_order(devices)
    place = {chip: at for at, chip in enumerate(order)}
    chips = len(order)

    def along(i, by):
        chip, core = divmod(i, 2)
        return order[(place[chip] + by) % chips] * 2 + core

    def turned(i, by):
        return along(i, by if i % 2 == 0 else -by)

    everyone = range(devices)
    return dict(
        up=[(i, along(i, 1)) for i in everyone],
        down=[(i, along(i, -1)) for i in everyone],
        turned=[(i, turned(i, 1)) for i in everyone],
        pair=[(i, i ^ 1) for i in everyone],
        after_up=[[along(i, -s) for s in range(chips)] for i in everyone],
    )


def attention_kernel(count, table, block_order, q_ref, *refs):
    key_refs, value_refs, out_ref = refs[:count], refs[count : 2 * count], refs[2 * count]
    rows = q_ref.shape[0]
    group = QUERY_HEADS // KEY_VALUE_HEADS
    row = lax.broadcasted_iota(jnp.int32, (rows, rows), 0)
    column = lax.broadcasted_iota(jnp.int32, (rows, rows), 1)
    places = [block_order[table[b]] * rows for b in range(count)]
    visible = jnp.concatenate([place + column <= places[0] + row for place in places], axis=1)
    scale = HEAD_SIZE ** (-0.5)
    for head in range(QUERY_HEADS):
        of = slice(head // group * HEAD_SIZE, (head // group + 1) * HEAD_SIZE)
        keys = jnp.concatenate([ref[:, of] for ref in key_refs], axis=0)
        values = jnp.concatenate([ref[:, of] for ref in value_refs], axis=0)
        query = q_ref[:, head * HEAD_SIZE : (head + 1) * HEAD_SIZE]
        scores = (
            lax.dot_general(
                query, keys, (((1,), (1,)), ((), ())), preferred_element_type=jnp.float32
            )
            * scale
        )
        scores = jnp.where(visible, scores, -jnp.inf)
        weights = jnp.exp(scores - jnp.max(scores, axis=1, keepdims=True))
        total = jnp.sum(weights, axis=1, keepdims=True)
        summed = jnp.dot(
            weights.astype(jnp.bfloat16), values, preferred_element_type=jnp.float32
        )
        out_ref[:, head * HEAD_SIZE : (head + 1) * HEAD_SIZE] = (summed / total).astype(
            jnp.bfloat16
        )


def attention(table, block_order, queries, keys, values):
    rows, width = queries.shape
    count = len(keys)
    return pl.pallas_call(
        functools.partial(attention_kernel, count),
        out_shape=jax.ShapeDtypeStruct((rows, width), jnp.bfloat16),
        in_specs=[pl.BlockSpec(memory_space=pltpu.SMEM)] * 2
        + [pl.BlockSpec(memory_space=pltpu.VMEM)] * (1 + 2 * count),
        out_specs=pl.BlockSpec(memory_space=pltpu.VMEM),
        cost_estimate=pl.CostEstimate(
            flops=4 * rows * rows * count * width,
            bytes_accessed=4 * rows * width + 4 * count * keys[0].size,
            transcendentals=rows * rows * count * QUERY_HEADS,
        ),
        name="attention",
    )(table, block_order, queries, *keys, *values)


def partial_kernel(parts, own_ref, other_ref, *refs):
    mine_ref, theirs_ref = refs[-2:]
    rows = own_ref.shape[0]
    out = 0.0
    done = start = 0
    for count in parts:
        blocks = refs[done : done + count]
        done += count
        at = slice(start, start + blocks[0].shape[0])
        start = at.stop
        context = jnp.concatenate([own_ref[:, at], other_ref[:, at]], axis=0)
        weight = jnp.concatenate([block[...] for block in blocks], axis=1)
        out += jnp.dot(context, weight, preferred_element_type=jnp.float32)
    mine_ref[...] = out[:rows]
    theirs_ref[...] = out[rows:]


def partial_product(own, other, parts):
    rows, depth = own.shape
    wide = sum(block.shape[1] for block in parts[0])
    blocks = [block for part in parts for block in part]
    return pl.pallas_call(
        functools.partial(partial_kernel, [len(part) for part in parts]),
        out_shape=(jax.ShapeDtypeStruct((rows, wide), jnp.float32),) * 2,
        in_specs=[pl.BlockSpec(memory_space=pltpu.VMEM)] * (2 + len(blocks)),
        out_specs=(pl.BlockSpec(memory_space=pltpu.VMEM),) * 2,
        cost_estimate=pl.CostEstimate(
            flops=4 * rows * depth * wide,
            bytes_accessed=2 * depth * wide + 4 * rows * depth,
            transcendentals=0,
        ),
        name="partial_product",
    )(own, other, *blocks)


def finish_kernel(wide, parts, skip, table, residual_ref, gain_ref, tags_ref, *refs):
    piece_refs = refs[: -1 - parts]
    updated_ref, normed_refs = refs[-1 - parts], refs[-parts:]
    done = skip
    for ref in piece_refs:
        for at in range(0, ref.shape[1], wide):
            to = pl.ds(pl.multiple_of(table[done] * wide, wide), wide)
            updated_ref[:, to] = residual_ref[:, to].astype(jnp.float32) + ref[:, at : at + wide]
            done += 1
    rows = updated_ref.shape[0] // parts
    for part, ref in enumerate(normed_refs):
        updated = updated_ref[part * rows : (part + 1) * rows]
        mean = jnp.mean(updated * updated, axis=1, keepdims=True)
        width = updated.shape[1]
        ref[:, :width] = (updated * lax.rsqrt(mean + 1e-06) * gain_ref[...]).astype(jnp.bfloat16)
        ref[:, width:] = tags_ref[part * rows : (part + 1) * rows]


def finish(table, skip, residual, gain, tags, pieces, parts):
    rows, width = residual.shape
    tagged = width + tags.shape[1]
    return pl.pallas_call(
        functools.partial(finish_kernel, width // (table.shape[0] - skip), parts, skip),
        out_shape=(jax.ShapeDtypeStruct((rows, width), jnp.float32),)
        + (jax.ShapeDtypeStruct((rows // parts, tagged), jnp.bfloat16),) * parts,
        in_specs=[pl.BlockSpec(memory_space=pltpu.SMEM)]
        + [pl.BlockSpec(memory_space=pltpu.VMEM)] * (3 + len(pieces)),
        out_specs=(pl.BlockSpec(memory_space=pltpu.VMEM),) * (1 + parts),
        cost_estimate=pl.CostEstimate(
            flops=6 * rows * width, bytes_accessed=12 * rows * width, transcendentals=rows
        ),
        name="finish",
    )(table, residual, gain.reshape(1, width), tags, *pieces)


def ringed(
    residual,
    queries,
    keys,
    values,
    block_order,
    routes,
    route_weights,
    out_weight,
    norm_gain,
    w_gate_up,
    w_down,
):
    rows = queries.shape[0]
    devices = lax.axis_size("ctx")
    own_index = lax.axis_index("ctx")
    ring = ring_tables(devices)
    chips = devices // 2
    half = chips // 2
    spans = range(devices // SEQS)
    turns = [0] + [t for s in range(1, half) for t in (s, chips - s)] + [half]

    def sent(array, way):
        return lax.ppermute(array, "ctx", ring[way])

    table = []
    for i in range(devices):
        columns = [ring["after_up"][i][t] for t in turns]
        table.append([(i - SEQS * s) % devices for s in spans] + columns + [c ^ 1 for c in columns])
    table = jnp.asarray(table, jnp.int32)[own_index]

    key_blocks = [keys] + [shifted(keys, "ctx", SEQS * s) for s in spans[1:]]
    value_blocks = [values] + [shifted(values, "ctx", SEQS * s) for s in spans[1:]]

    gates = route_weights / jnp.sum(route_weights, axis=-1, keepdims=True)
    named = routes[:, :, None] == jnp.arange(devices, dtype=jnp.int32)
    left = jnp.sum(jnp.where(named, gates[:, :, None], 0.0), axis=1)
    addends = []
    for _ in range(3):
        addends.append(lax.reduce_precision(left, 8, 7))
        left = left - addends[-1]
    tags = jnp.concatenate(addends, axis=1).astype(jnp.bfloat16)
    tags = jnp.pad(tags, ((0, 0), (0, -tags.shape[1] % 128)))

    depth = out_weight.shape[0] // 2
    up = down = whole = (out_weight[:depth], out_weight[depth:])
    rounds = []
    for _ in range(1, half):
        up = tuple(sent(part, "up") for part in up)
        down = tuple(sent(part, "down") for part in down)
        rounds.append([up, down])
    context = attention(table, block_order, queries, key_blocks, value_blocks)
    rounds.append([(sent(up[0], "up"), sent(down[1], "down"))])
    other_context = sent(context, "pair")
    pieces, away = [], []
    early = [whole] + [block for got in rounds[:-2] for block in got]
    for got in [early] + rounds[-2:]:
        mine, theirs = partial_product(context, other_context, list(zip(*got)))
        pieces.append(mine)
        away.append(sent(theirs, "pair"))
    updated, *normed = finish(table, len(spans), residual, norm_gain, tags, pieces + away, PARTS)

    lane = jnp.arange(tags.shape[1])
    own_lane = (lane % devices == own_index) & (lane < 3 * devices)
    picks = jnp.broadcast_to(own_lane[:, None], (lane.shape[0], 128)).astype(jnp.bfloat16)
    moving = normed
    summed = None
    for step in range(chips):
        if step > 0:
            moving = [sent(part, "turned") for part in moving]
        both = jnp.concatenate([*moving, *[sent(part, "pair") for part in moving]], axis=0)
        width = both.shape[1] - lane.shape[0]
        hidden = jnp.dot(both[:, :width], w_gate_up[0], preferred_element_type=jnp.float32)
        hidden = (jax.nn.silu(hidden[:, :FF]) * hidden[:, FF:]).astype(jnp.bfloat16)
        out = jnp.dot(hidden, w_down[0], preferred_element_type=jnp.float32).astype(jnp.bfloat16)
        gate = jnp.dot(both[:, width:], picks, preferred_element_type=jnp.float32)[:, :1]
        out = jnp.where(gate > 0.0, gate * out.astype(jnp.float32), 0.0)
        theirs = sent(out[rows:].astype(jnp.bfloat16), "pair")
        total = out[:rows] + theirs.astype(jnp.float32)
        if step == 0:
            first = updated + total
            continue
        cuts = [] if step < chips - TAIL else [5 * rows // 8]
        totals = jnp.split(total, cuts)
        if summed is not None:
            if len(summed) < len(totals):
                summed = jnp.split(summed[0], cuts)
            totals = [t + s.astype(jnp.float32) for t, s in zip(totals, summed)]
        summed = [sent(t.astype(jnp.bfloat16), "turned") for t in totals]
    mixed = first + jnp.concatenate(summed).astype(jnp.float32)
    return (context, mixed.astype(jnp.bfloat16))


def local(*arrays):
    devices = lax.axis_size("ctx")
    held_experts = arrays[9].shape[0]
    if held_experts == 1 and devices <= 2 * TOPK and devices % (2 * SEQS) == 0:
        return ringed(*arrays)
    return exchanged(*arrays)


def solution(mesh):
    placed = (
        P(("groups", "ctx"), None),
        P(("groups", "ctx"), None),
        P(("groups", "ctx"), None),
        P(("groups", "ctx"), None),
        P("groups"),
        P(("groups", "ctx"), None),
        P(("groups", "ctx"), None),
        P(None, "ctx"),
        P(),
        P("ctx", None, None),
        P("ctx", None, None),
    )
    return jax.shard_map(
        local,
        mesh=mesh,
        in_specs=placed,
        out_specs=(P(("groups", "ctx"), None), P(("groups", "ctx"), None)),
        check_vma=False,
    )
```

```python
import functools

import jax
import jax.numpy as jnp
from jax import lax
from jax.experimental import pallas as pl
from jax.experimental.pallas import tpu as pltpu
from jax.sharding import PartitionSpec as P


D = 2048
HEAD_SIZE = 128
FF = 768
QUERY_HEADS = 16
KEY_VALUE_HEADS = 2
TOPK = 8
SEQS = 4
KERNEL_BYTES = 16 << 20
PARTS = 1
TAIL = 3


def shifted(array, axis, by):
    devices = lax.axis_size(axis)
    return lax.ppermute(array, axis, [(i, (i + by) % devices) for i in range(devices)])


def exchanged(
    residual,
    queries,
    keys,
    values,
    block_order,
    routes,
    route_weights,
    out_weight,
    norm_gain,
    w_gate_up,
    w_down,
):
    device_row_count = queries.shape[0]
    query_group_width = QUERY_HEADS // KEY_VALUE_HEADS
    devices = lax.axis_size("ctx")
    cycle_length = devices // SEQS
    own_index = lax.axis_index("ctx")
    full_weight = lax.all_gather(out_weight, "ctx", axis=1, tiled=True)
    query_position = block_order[own_index]
    query_head_rows = (
        queries.reshape(device_row_count, KEY_VALUE_HEADS, query_group_width, HEAD_SIZE)
        .transpose(1, 2, 0, 3)
        .reshape(KEY_VALUE_HEADS, query_group_width * device_row_count, HEAD_SIZE)
    )
    query_offset = jnp.arange(query_group_width * device_row_count) % device_row_count
    key_offset = jnp.arange(device_row_count)
    scale = HEAD_SIZE ** (-0.5)

    def update(carry, key_value_tuple, key_position):
        summed, running_max, totals = carry
        local_key_block = key_value_tuple[0].reshape(device_row_count, KEY_VALUE_HEADS, HEAD_SIZE)
        local_value_block = key_value_tuple[1].reshape(device_row_count, KEY_VALUE_HEADS, HEAD_SIZE)
        scores = (
            jnp.einsum(
                "hqd,khd->hqk", query_head_rows, local_key_block, preferred_element_type=jnp.float32
            )
            * scale
        )
        visible = (
            key_position * device_row_count + key_offset[None, :]
            <= query_position * device_row_count + query_offset[:, None]
        )
        scores = jnp.where(visible[None], scores, -jnp.inf)
        new_max = jnp.maximum(running_max, jnp.max(scores, axis=-1))
        factor = jnp.exp(running_max - new_max)
        weights = jnp.exp(scores - new_max[..., None])
        totals = totals * factor + jnp.sum(weights, axis=-1)
        summed = summed * factor[..., None] + jnp.einsum(
            "hqk,khd->hqd",
            weights.astype(jnp.bfloat16),
            local_value_block,
            preferred_element_type=jnp.float32,
        )
        return (summed, new_max, totals)

    initial = (
        jnp.zeros((KEY_VALUE_HEADS, query_group_width * device_row_count, HEAD_SIZE), jnp.float32),
        jnp.full((KEY_VALUE_HEADS, query_group_width * device_row_count), -jnp.inf, jnp.float32),
        jnp.zeros((KEY_VALUE_HEADS, query_group_width * device_row_count), jnp.float32),
    )
    local_pair = jnp.stack([keys, values])
    carry = update(initial, local_pair, query_position)

    def advance(step, state):
        current, moving = state
        moving = shifted(moving, "ctx", SEQS)
        anchor = jnp.mod(own_index - SEQS * step, devices)
        key_position = block_order[anchor]
        current = lax.cond(
            key_position <= query_position,
            lambda inner: update(inner, moving, key_position),
            lambda inner: inner,
            current,
        )
        return (current, moving)

    carry, _ = lax.fori_loop(1, cycle_length, advance, (carry, local_pair))
    summed, _, totals = carry
    context = (
        (summed / totals[..., None])
        .reshape(KEY_VALUE_HEADS, query_group_width, device_row_count, HEAD_SIZE)
        .transpose(2, 0, 1, 3)
        .reshape(device_row_count, QUERY_HEADS * HEAD_SIZE)
        .astype(jnp.bfloat16)
    )
    projected = jnp.dot(context, full_weight, preferred_element_type=jnp.float32)
    updated = residual.astype(jnp.float32) + projected
    normed = (
        updated * lax.rsqrt(jnp.mean(updated * updated, axis=-1, keepdims=True) + 1e-06) * norm_gain
    ).astype(jnp.bfloat16)
    experts = devices * w_gate_up.shape[0]
    capacity = 9 * device_row_count * TOPK // (8 * experts)
    expert_ids = routes.reshape(-1)
    one_hot = (expert_ids[:, None] == jnp.arange(experts, dtype=jnp.int32)[None, :]).astype(
        jnp.int32
    )
    ranks = jnp.sum(jnp.cumsum(one_hot, axis=0) * one_hot, axis=1) - 1
    target = expert_ids * capacity + ranks
    source_row = jnp.arange(device_row_count * TOPK) // TOPK
    outgoing = (
        jnp.zeros((experts * capacity, D), jnp.bfloat16)
        .at[target]
        .set(normed[source_row])
        .reshape(experts, capacity, D)
    )
    arrived = lax.all_to_all(outgoing, "ctx", split_axis=0, concat_axis=0, tiled=True)
    flat = arrived.reshape(-1, D)
    both = jnp.dot(flat, w_gate_up[0], preferred_element_type=jnp.float32)
    hidden = (jax.nn.silu(both[:, :FF]) * both[:, FF:]).astype(jnp.bfloat16)
    result = (
        jnp.dot(hidden, w_down[0], preferred_element_type=jnp.float32)
        .astype(jnp.bfloat16)
        .reshape(arrived.shape)
    )
    returned = lax.all_to_all(result, "ctx", split_axis=0, concat_axis=0, tiled=True)
    gathered = returned.reshape(-1, D)[target].reshape(device_row_count, TOPK, D)
    gates = route_weights / jnp.sum(route_weights, axis=-1, keepdims=True)
    mixed = updated
    for slot in range(TOPK):
        mixed = mixed + gates[:, slot : slot + 1] * gathered[:, slot].astype(jnp.float32)
    return (context, mixed.astype(jnp.bfloat16))


def ring_order(devices):
    chips = devices // 2
    return list(range(0, chips, 2)) + list(range(chips - 1, 0, -2))


def ring_tables(devices):
    order = ring_order(devices)
    place = {chip: at for at, chip in enumerate(order)}
    chips = len(order)

    def along(i, by):
        chip, core = divmod(i, 2)
        return order[(place[chip] + by) % chips] * 2 + core

    def turned(i, by):
        return along(i, by if i % 2 == 0 else -by)

    everyone = range(devices)
    return dict(
        up=[(i, along(i, 1)) for i in everyone],
        down=[(i, along(i, -1)) for i in everyone],
        turned=[(i, turned(i, 1)) for i in everyone],
        pair=[(i, i ^ 1) for i in everyone],
        after_up=[[along(i, -s) for s in range(chips)] for i in everyone],
    )


def attention_kernel(count, table, block_order, q_ref, *refs):
    key_refs, value_refs, out_ref = refs[:count], refs[count : 2 * count], refs[2 * count]
    rows = q_ref.shape[0]
    group = QUERY_HEADS // KEY_VALUE_HEADS
    row = lax.broadcasted_iota(jnp.int32, (rows, rows), 0)
    column = lax.broadcasted_iota(jnp.int32, (rows, rows), 1)
    places = [block_order[table[b]] * rows for b in range(count)]
    visible = jnp.concatenate([place + column <= places[0] + row for place in places], axis=1)
    scale = HEAD_SIZE ** (-0.5)
    for head in range(QUERY_HEADS):
        of = slice(head // group * HEAD_SIZE, (head // group + 1) * HEAD_SIZE)
        keys = jnp.concatenate([ref[:, of] for ref in key_refs], axis=0)
        values = jnp.concatenate([ref[:, of] for ref in value_refs], axis=0)
        query = q_ref[:, head * HEAD_SIZE : (head + 1) * HEAD_SIZE]
        scores = (
            lax.dot_general(
                query, keys, (((1,), (1,)), ((), ())), preferred_element_type=jnp.float32
            )
            * scale
        )
        scores = jnp.where(visible, scores, -jnp.inf)
        weights = jnp.exp(scores - jnp.max(scores, axis=1, keepdims=True))
        total = jnp.sum(weights, axis=1, keepdims=True)
        summed = jnp.dot(
            weights.astype(jnp.bfloat16), values, preferred_element_type=jnp.float32
        )
        out_ref[:, head * HEAD_SIZE : (head + 1) * HEAD_SIZE] = (summed / total).astype(
            jnp.bfloat16
        )


def attention(table, block_order, queries, keys, values):
    rows, width = queries.shape
    count = len(keys)
    return pl.pallas_call(
        functools.partial(attention_kernel, count),
        out_shape=jax.ShapeDtypeStruct((rows, width), jnp.bfloat16),
        in_specs=[pl.BlockSpec(memory_space=pltpu.SMEM)] * 2
        + [pl.BlockSpec(memory_space=pltpu.VMEM)] * (1 + 2 * count),
        out_specs=pl.BlockSpec(memory_space=pltpu.VMEM),
        cost_estimate=pl.CostEstimate(
            flops=4 * rows * rows * count * width,
            bytes_accessed=4 * rows * width + 4 * count * keys[0].size,
            transcendentals=rows * rows * count * QUERY_HEADS,
        ),
        compiler_params=pltpu.CompilerParams(vmem_limit_bytes=KERNEL_BYTES),
        name="attention",
    )(table, block_order, queries, *keys, *values)


def partial_kernel(parts, own_ref, other_ref, *refs):
    mine_ref, theirs_ref = refs[-2:]
    rows = own_ref.shape[0]
    out = 0.0
    done = start = 0
    for count in parts:
        blocks = refs[done : done + count]
        done += count
        at = slice(start, start + blocks[0].shape[0])
        start = at.stop
        context = jnp.concatenate([own_ref[:, at], other_ref[:, at]], axis=0)
        weight = jnp.concatenate([block[...] for block in blocks], axis=1)
        out += jnp.dot(context, weight, preferred_element_type=jnp.float32)
    mine_ref[...] = out[:rows]
    theirs_ref[...] = out[rows:]


def partial_product(own, other, parts):
    rows, depth = own.shape
    wide = sum(block.shape[1] for block in parts[0])
    blocks = [block for part in parts for block in part]
    return pl.pallas_call(
        functools.partial(partial_kernel, [len(part) for part in parts]),
        out_shape=(jax.ShapeDtypeStruct((rows, wide), jnp.float32),) * 2,
        in_specs=[pl.BlockSpec(memory_space=pltpu.VMEM)] * (2 + len(blocks)),
        out_specs=(pl.BlockSpec(memory_space=pltpu.VMEM),) * 2,
        cost_estimate=pl.CostEstimate(
            flops=4 * rows * depth * wide,
            bytes_accessed=2 * depth * wide + 4 * rows * depth,
            transcendentals=0,
        ),
        name="partial_product",
    )(own, other, *blocks)


def finish_kernel(wide, parts, skip, table, residual_ref, gain_ref, tags_ref, *refs):
    piece_refs = refs[: -1 - parts]
    updated_ref, normed_refs = refs[-1 - parts], refs[-parts:]
    done = skip
    for ref in piece_refs:
        for at in range(0, ref.shape[1], wide):
            to = pl.ds(pl.multiple_of(table[done] * wide, wide), wide)
            updated_ref[:, to] = residual_ref[:, to].astype(jnp.float32) + ref[:, at : at + wide]
            done += 1
    rows = updated_ref.shape[0] // parts
    for part, ref in enumerate(normed_refs):
        updated = updated_ref[part * rows : (part + 1) * rows]
        mean = jnp.mean(updated * updated, axis=1, keepdims=True)
        width = updated.shape[1]
        ref[:, :width] = (updated * lax.rsqrt(mean + 1e-06) * gain_ref[...]).astype(jnp.bfloat16)
        ref[:, width:] = tags_ref[part * rows : (part + 1) * rows]


def finish(table, skip, residual, gain, tags, pieces, parts):
    rows, width = residual.shape
    tagged = width + tags.shape[1]
    return pl.pallas_call(
        functools.partial(finish_kernel, width // (table.shape[0] - skip), parts, skip),
        out_shape=(jax.ShapeDtypeStruct((rows, width), jnp.float32),)
        + (jax.ShapeDtypeStruct((rows // parts, tagged), jnp.bfloat16),) * parts,
        in_specs=[pl.BlockSpec(memory_space=pltpu.SMEM)]
        + [pl.BlockSpec(memory_space=pltpu.VMEM)] * (3 + len(pieces)),
        out_specs=(pl.BlockSpec(memory_space=pltpu.VMEM),) * (1 + parts),
        cost_estimate=pl.CostEstimate(
            flops=6 * rows * width, bytes_accessed=12 * rows * width, transcendentals=rows
        ),
        compiler_params=pltpu.CompilerParams(vmem_limit_bytes=KERNEL_BYTES),
        name="finish",
    )(table, residual, gain.reshape(1, width), tags, *pieces)


def ringed(
    residual,
    queries,
    keys,
    values,
    block_order,
    routes,
    route_weights,
    out_weight,
    norm_gain,
    w_gate_up,
    w_down,
):
    rows = queries.shape[0]
    devices = lax.axis_size("ctx")
    own_index = lax.axis_index("ctx")
    ring = ring_tables(devices)
    chips = devices // 2
    half = chips // 2
    spans = range(devices // SEQS)
    turns = [0] + [t for s in range(1, half) for t in (s, chips - s)] + [half]

    def sent(array, way):
        return lax.ppermute(array, "ctx", ring[way])

    table = []
    for i in range(devices):
        columns = [ring["after_up"][i][t] for t in turns]
        table.append([(i - SEQS * s) % devices for s in spans] + columns + [c ^ 1 for c in columns])
    table = jnp.asarray(table, jnp.int32)[own_index]

    key_blocks = [keys] + [shifted(keys, "ctx", SEQS * s) for s in spans[1:]]
    value_blocks = [values] + [shifted(values, "ctx", SEQS * s) for s in spans[1:]]

    gates = route_weights / jnp.sum(route_weights, axis=-1, keepdims=True)
    named = routes[:, :, None] == jnp.arange(devices, dtype=jnp.int32)
    left = jnp.sum(jnp.where(named, gates[:, :, None], 0.0), axis=1)
    addends = []
    for _ in range(3):
        addends.append(lax.reduce_precision(left, 8, 7))
        left = left - addends[-1]
    tags = jnp.concatenate(addends, axis=1).astype(jnp.bfloat16)
    tags = jnp.pad(tags, ((0, 0), (0, -tags.shape[1] % 128)))

    depth = out_weight.shape[0] // 2
    up = down = whole = (out_weight[:depth], out_weight[depth:])
    rounds = []
    for _ in range(1, half):
        up = tuple(sent(part, "up") for part in up)
        down = tuple(sent(part, "down") for part in down)
        rounds.append([up, down])
    context = attention(table, block_order, queries, key_blocks, value_blocks)
    rounds.append([(sent(up[0], "up"), sent(down[1], "down"))])
    other_context = sent(context, "pair")
    pieces, away = [], []
    early = [whole] + [block for got in rounds[:-2] for block in got]
    for step, got in enumerate([early] + rounds[-2:]):
        if step < half - 2:
            mine, theirs = partial_product(context, other_context, list(zip(*got)))
        else:
            both = jnp.concatenate([context, other_context], axis=0)
            product, start = 0.0, 0
            for part in got[0]:
                rows_in = both[:, start : start + part.shape[0]]
                product += jnp.dot(rows_in, part, preferred_element_type=jnp.float32)
                start += part.shape[0]
            mine, theirs = product[:rows], product[rows:]
        pieces.append(mine)
        away.append(sent(theirs, "pair"))
    updated, *normed = finish(table, len(spans), residual, norm_gain, tags, pieces + away, PARTS)

    lane = jnp.arange(tags.shape[1])
    own_lane = (lane % devices == own_index) & (lane < 3 * devices)
    picks = jnp.broadcast_to(own_lane[:, None], (lane.shape[0], 128)).astype(jnp.bfloat16)
    moving = normed
    summed = None
    for step in range(chips):
        if step > 0:
            moving = [sent(part, "turned") for part in moving]
        both = jnp.concatenate([*moving, *[sent(part, "pair") for part in moving]], axis=0)
        width = both.shape[1] - lane.shape[0]
        hidden = jnp.dot(both[:, :width], w_gate_up[0], preferred_element_type=jnp.float32)
        hidden = (jax.nn.silu(hidden[:, :FF]) * hidden[:, FF:]).astype(jnp.bfloat16)
        out = jnp.dot(hidden, w_down[0], preferred_element_type=jnp.float32).astype(jnp.bfloat16)
        gate = jnp.dot(both[:, width:], picks, preferred_element_type=jnp.float32)[:, :1]
        out = jnp.where(gate > 0.0, gate * out.astype(jnp.float32), 0.0)
        theirs = sent(out[rows:].astype(jnp.bfloat16), "pair")
        total = out[:rows] + theirs.astype(jnp.float32)
        if step == 0:
            first = updated + total
            continue
        cuts = [] if step < chips - TAIL else [5 * rows // 8]
        totals = jnp.split(total, cuts)
        if summed is not None:
            if len(summed) < len(totals):
                summed = jnp.split(summed[0], cuts)
            totals = [t + s.astype(jnp.float32) for t, s in zip(totals, summed)]
        summed = [sent(t.astype(jnp.bfloat16), "turned") for t in totals]
    mixed = first + jnp.concatenate(summed).astype(jnp.float32)
    return (context, mixed.astype(jnp.bfloat16))


def local(*arrays):
    devices = lax.axis_size("ctx")
    held_experts = arrays[9].shape[0]
    if held_experts == 1 and devices <= 2 * TOPK and devices % (2 * SEQS) == 0:
        return ringed(*arrays)
    return exchanged(*arrays)


def solution(mesh):
    placed = (
        P(("groups", "ctx"), None),
        P(("groups", "ctx"), None),
        P(("groups", "ctx"), None),
        P(("groups", "ctx"), None),
        P("groups"),
        P(("groups", "ctx"), None),
        P(("groups", "ctx"), None),
        P(None, "ctx"),
        P(),
        P("ctx", None, None),
        P("ctx", None, None),
    )
    return jax.shard_map(
        local,
        mesh=mesh,
        in_specs=placed,
        out_specs=(P(("groups", "ctx"), None), P(("groups", "ctx"), None)),
        check_vma=False,
    )
```
